32 devices in a mesh: groups: 2 (over x), spatial: 16 (over z, y, core).
Axes of the slice: x: 2, y: 2, z: 4, core: 2. Of those that a mesh axis runs over, the one named last changes fastest.
Arguments:
- fields: bfloat16 [1024, 128, 768], P(('groups', 'spatial')), parts along dimension 0, may hold values from -6 to 6
- norm1_gain: float32 [768], replicated, may hold values from 0.5 to 1.5
- norm1_bias: float32 [768], replicated, may hold values from -3 to 3
- spectral_w1: float32 [2, 8, 96, 96], replicated, may hold values from -0.4375 to 0.4375
- spectral_b1: float32 [2, 8, 96], replicated, may hold values from -3 to 3
- spectral_w2: float32 [2, 8, 96, 96], replicated, may hold values from -0.4375 to 0.4375
- spectral_b2: float32 [2, 8, 96], replicated, may hold values from -3 to 3
- norm2_gain: float32 [768], replicated, may hold values from 0.5 to 1.5
- norm2_bias: float32 [768], replicated, may hold values from -3 to 3
- fc1_weight: bfloat16 [768, 3072], replicated, may hold values from -0.21875 to 0.21875
- fc1_bias: float32 [3072], replicated, may hold values from -3 to 3
- fc2_weight: bfloat16 [3072, 768], replicated, may hold values from -0.109375 to 0.109375
- fc2_bias: float32 [768], replicated, may hold values from -3 to 3
Outputs:
- next_state: bfloat16 [1024, 128, 768], P(('groups', 'spatial')), parts along dimension 0
- anomaly: bfloat16 [1024, 128, 768], P(('groups', 'spatial')), parts along dimension 0
The draws below stay inside these ranges and needn't reach their ends.
There are 2 independent parts, one for each index of `groups`. The reference program is written for one: setup_inputs(seed, part) draws one part's arguments, and reference() takes and returns one part's arrays. A program takes and returns all parts, laid end to end along the dimension named above; an argument that names none is the same for every part. Nothing has to cross between parts.
All inputs are finite; a program needn't handle non-finite values.
Results may differ from the reference program's by a relative error of at most 0.0056.
Values may be sent and summed in bfloat16 or wider, within the bound.
A program may use at most 192 MiB of HBM per device.

```python
import jax
import jax.numpy as jnp
from jax import lax

D = 768
FF = 3072
NB = 8
BS = 96
LAT = 64
LON = 128
MEMBERS = 8


def block_levels(key, shape, cuts, least, top_value):
    loudness = 1.0
    for dim, shards_of in cuts:
        draws = jax.random.uniform(jax.random.fold_in(jax.random.fold_in(key, 6), dim), (shards_of,), jnp.float32, least / len(cuts), top_value / len(cuts))
        loudness = loudness * jnp.repeat(jnp.exp(draws), shape[dim] // shards_of).reshape((-1,) + (1,) * (len(shape) - 1 - dim))
    return loudness


def noise(stream_key, dims, scale, reach, shards=(), dtype=jnp.bfloat16):
    values = jax.random.normal(stream_key, dims, jnp.float32) * scale
    if len(shards) > 0:
        values = block_levels(stream_key, dims, shards, -0.22, 0.18) * values
    return jnp.clip(values, min=-reach, max=reach).astype(dtype)


def setup_inputs(seed: int = 0, part: int = 0) -> dict:
    key_list = jax.random.split(jax.random.key(seed), 14)
    part_keys = jax.random.split(jax.random.fold_in(key_list[13], part), 14)
    return {
        "fields": noise(part_keys[0], (MEMBERS * LAT, LON, D), 1.0, 6.0, ((0, 16),)),
        "norm1_gain": jnp.clip(1.0 + 0.1 * jax.random.normal(key_list[1], (D,), jnp.float32), 0.5, 1.5),
        "norm1_bias": noise(key_list[2], (D,), 0.5, 3.0, (), jnp.float32),
        "spectral_w1": noise(key_list[3], (2, NB, BS, BS), (2 * BS) ** -0.5, 0.4375, (), jnp.float32),
        "spectral_b1": noise(key_list[4], (2, NB, BS), 0.5, 3.0, (), jnp.float32),
        "spectral_w2": noise(key_list[5], (2, NB, BS, BS), (2 * BS) ** -0.5, 0.4375, (), jnp.float32),
        "spectral_b2": noise(key_list[6], (2, NB, BS), 0.5, 3.0, (), jnp.float32),
        "norm2_gain": jnp.clip(1.0 + 0.1 * jax.random.normal(key_list[7], (D,), jnp.float32), 0.5, 1.5),
        "norm2_bias": noise(key_list[8], (D,), 0.5, 3.0, (), jnp.float32),
        "fc1_weight": noise(key_list[9], (D, FF), D ** -0.5, 0.21875),
        "fc1_bias": noise(key_list[10], (FF,), 0.5, 3.0, (), jnp.float32),
        "fc2_weight": noise(key_list[11], (FF, D), FF ** -0.5, 0.109375),
        "fc2_bias": noise(key_list[12], (D,), 0.5, 3.0, (), jnp.float32),
    }


EPSILON = 1e-06
SHRINK = 0.01
FULL_PRECISION = lax.Precision.HIGHEST

def layer_norm(values, gain, offset_term):
    center = values - lax.optimization_barrier(jnp.mean(values, axis=-1, keepdims=True))
    spread = lax.optimization_barrier(jnp.mean(center * center, axis=-1, keepdims=True))
    return center * lax.rsqrt(spread + EPSILON) * gain + offset_term

def soft_shrink(values):
    return jnp.where(values > SHRINK, values - SHRINK, jnp.where(values < -SHRINK, values + SHRINK, 0.0))

def block_product(values, weight):
    return jnp.einsum('...bi,bio->...bo', values, weight, precision=FULL_PRECISION)

def spectral_layer(real_part, imag_part, w_first, b_first, w_second, b_second):
    shape = real_part.shape
    block_count = w_first.shape[1]
    split_shape = shape[:-1] + (block_count, shape[-1] // block_count)
    real_part = real_part.reshape(split_shape)
    imag_part = imag_part.reshape(split_shape)
    hidden_real = jax.nn.relu(block_product(real_part, w_first[0]) - block_product(imag_part, w_first[1]) + b_first[0])
    hidden_imag = jax.nn.relu(block_product(imag_part, w_first[0]) + block_product(real_part, w_first[1]) + b_first[1])
    mixed_real = block_product(hidden_real, w_second[0]) - block_product(hidden_imag, w_second[1]) + b_second[0]
    mixed_imag = block_product(hidden_imag, w_second[0]) + block_product(hidden_real, w_second[1]) + b_second[1]
    return (soft_shrink(mixed_real).reshape(shape), soft_shrink(mixed_imag).reshape(shape))

def reference(fields, norm1_gain, norm1_bias, spectral_w1, spectral_b1, spectral_w2, spectral_b2, norm2_gain, norm2_bias, fc1_weight, fc1_bias, fc2_weight, fc2_bias):
    state = fields.astype(jnp.float32).reshape(MEMBERS, LAT, LON, D)
    normed = layer_norm(state, norm1_gain, norm1_bias)
    spectrum = jnp.fft.rfft2(normed, axes=(1, 2), norm='ortho')[:, :, :LON // 2, :]
    mixed_real, mixed_imag = spectral_layer(jnp.real(spectrum), jnp.imag(spectrum), spectral_w1, spectral_b1, spectral_w2, spectral_b2)
    kept = mixed_real + 1j * mixed_imag
    padded = jnp.concatenate([kept, jnp.zeros_like(kept[:, :, :1, :])], axis=2)
    filtered = jnp.fft.irfft2(padded, s=(LAT, LON), axes=(1, 2), norm='ortho')
    residual = (filtered + normed + state).reshape(MEMBERS * LAT * LON, D)
    normed2 = layer_norm(residual, norm2_gain, norm2_bias).astype(jnp.bfloat16)
    hidden = jax.nn.gelu(jnp.dot(normed2, fc1_weight, preferred_element_type=jnp.float32) + fc1_bias, approximate=False).astype(jnp.bfloat16)
    updated = residual + jnp.dot(hidden, fc2_weight, preferred_element_type=jnp.float32) + fc2_bias
    next_state = updated.astype(jnp.bfloat16)
    member_values = next_state.astype(jnp.float32).reshape(MEMBERS, LAT * LON, D)
    ensemble_mean = lax.optimization_barrier(jnp.sum(member_values, axis=0)) / MEMBERS
    anomaly = (member_values - ensemble_mean).astype(jnp.bfloat16)
    return (next_state.reshape(MEMBERS * LAT, LON, D), anomaly.reshape(MEMBERS * LAT, LON, D))
```

```python
import math

import jax
import jax.numpy as jnp
from jax import lax
from jax.sharding import Mesh, PartitionSpec as P

MEMBERS = 8


EPSILON = 1e-06
SHRINK = 0.01
FULL_PRECISION = lax.Precision.HIGHEST


def from_behind(block, axis, distance):
    devices = range(lax.axis_size(axis))
    route = [((i - distance) % len(devices), i) for i in devices]
    return lax.ppermute(block, axis, route)


def layer_norm(values, gain, offset_term):
    center = values - jnp.mean(values, axis=-1, keepdims=True)
    spread = jnp.mean(center * center, axis=-1, keepdims=True)
    return center * lax.rsqrt(spread + EPSILON) * gain + offset_term


def soft_shrink(values):
    return jnp.where(
        values > SHRINK, values - SHRINK, jnp.where(values < -SHRINK, values + SHRINK, 0.0)
    )


def contract(form, left, right):
    return jnp.einsum(form, left, right, precision=FULL_PRECISION)


def block_product(values, weight):
    return jnp.einsum("...bi,bio->...bo", values, weight, precision=FULL_PRECISION)


def angle_table(first_len, second_len, modulus):
    first_index = lax.broadcasted_iota(jnp.int32, (first_len, second_len), 0)
    second_index = lax.broadcasted_iota(jnp.int32, (first_len, second_len), 1)
    phase = first_index * second_index % modulus
    return phase.astype(jnp.float32) * (2.0 * math.pi / modulus)


def spectral_layer(real_part, imag_part, w_first, b_first, w_second, b_second):
    shape = real_part.shape
    block_count = w_first.shape[1]
    split_shape = shape[:-1] + (block_count, shape[-1] // block_count)
    real_part = real_part.reshape(split_shape)
    imag_part = imag_part.reshape(split_shape)
    hidden_real = jax.nn.relu(
        block_product(real_part, w_first[0]) - block_product(imag_part, w_first[1]) + b_first[0]
    )
    hidden_imag = jax.nn.relu(
        block_product(imag_part, w_first[0]) + block_product(real_part, w_first[1]) + b_first[1]
    )
    mixed_real = (
        block_product(hidden_real, w_second[0])
        - block_product(hidden_imag, w_second[1])
        + b_second[0]
    )
    mixed_imag = (
        block_product(hidden_imag, w_second[0])
        + block_product(hidden_real, w_second[1])
        + b_second[1]
    )
    return (soft_shrink(mixed_real).reshape(shape), soft_shrink(mixed_imag).reshape(shape))


def longitude_forward(normed, lon_len):
    angles = angle_table(lon_len, lon_len // 2, lon_len)
    factor = 1.0 / math.sqrt(lon_len)
    real_part = contract("rld,lk->rkd", normed, jnp.cos(angles) * factor)
    imag_part = -contract("rld,lk->rkd", normed, jnp.sin(angles) * factor)
    return (real_part, imag_part)


def longitude_inverse(real_part, imag_part, lon_len):
    half_len = lon_len // 2
    angles = angle_table(lon_len, half_len, lon_len)
    column_index = lax.broadcasted_iota(jnp.int32, (1, half_len), 1)
    weights = jnp.where(column_index == 0, 1.0, 2.0) / math.sqrt(lon_len)
    cosine_table = jnp.cos(angles) * weights
    sine_table = jnp.sin(angles) * weights
    return contract("rkd,lk->rld", real_part, cosine_table) - contract(
        "rkd,lk->rld", imag_part, sine_table
    )


def latitude_work(real_part, imag_part, w_first, b_first, w_second, b_second):
    member_rows, mode_count, channels = real_part.shape
    lat_len = member_rows // MEMBERS
    angles = angle_table(lat_len, lat_len, lat_len)
    factor = 1.0 / math.sqrt(lat_len)
    cosine_table = jnp.cos(angles) * factor
    sine_table = jnp.sin(angles) * factor
    grid_real = real_part.reshape(MEMBERS, lat_len, mode_count, channels)
    grid_imag = imag_part.reshape(MEMBERS, lat_len, mode_count, channels)
    spec_real = contract("qp,mpkd->mqkd", cosine_table, grid_real) + contract(
        "qp,mpkd->mqkd", sine_table, grid_imag
    )
    spec_imag = contract("qp,mpkd->mqkd", cosine_table, grid_imag) - contract(
        "qp,mpkd->mqkd", sine_table, grid_real
    )
    mixed_real, mixed_imag = spectral_layer(
        spec_real, spec_imag, w_first, b_first, w_second, b_second
    )
    back_real = contract("qp,mpkd->mqkd", cosine_table, mixed_real) - contract(
        "qp,mpkd->mqkd", sine_table, mixed_imag
    )
    back_imag = contract("qp,mpkd->mqkd", cosine_table, mixed_imag) + contract(
        "qp,mpkd->mqkd", sine_table, mixed_real
    )
    return (
        back_real.reshape(member_rows, mode_count, channels),
        back_imag.reshape(member_rows, mode_count, channels),
    )


def on_device(
    fields,
    norm1_gain,
    norm1_bias,
    spectral_w1,
    spectral_b1,
    spectral_w2,
    spectral_b2,
    norm2_gain,
    norm2_bias,
    fc1_weight,
    fc1_bias,
    fc2_weight,
    fc2_bias,
):
    row_count, lon_len, channels = fields.shape
    state = fields.astype(jnp.float32)
    normed = layer_norm(state, norm1_gain, norm1_bias)
    real_part, imag_part = longitude_forward(normed, lon_len)
    real_part, imag_part = (
        lax.all_to_all(real_part, "spatial", split_axis=1, concat_axis=0, tiled=True),
        lax.all_to_all(imag_part, "spatial", split_axis=1, concat_axis=0, tiled=True),
    )
    real_part, imag_part = latitude_work(
        real_part, imag_part, spectral_w1, spectral_b1, spectral_w2, spectral_b2
    )
    real_part, imag_part = (
        lax.all_to_all(real_part, "spatial", split_axis=0, concat_axis=1, tiled=True),
        lax.all_to_all(imag_part, "spatial", split_axis=0, concat_axis=1, tiled=True),
    )
    filtered = longitude_inverse(real_part, imag_part, lon_len)
    residual = (filtered + normed + state).reshape(row_count * lon_len, channels)
    normed2 = layer_norm(residual, norm2_gain, norm2_bias).astype(jnp.bfloat16)
    hidden = jax.nn.gelu(
        jnp.dot(normed2, fc1_weight, preferred_element_type=jnp.float32) + fc1_bias,
        approximate=False,
    ).astype(jnp.bfloat16)
    updated = residual + jnp.dot(hidden, fc2_weight, preferred_element_type=jnp.float32) + fc2_bias
    next_state = updated.astype(jnp.bfloat16).reshape(row_count, lon_len, channels)
    return next_state


def ensemble_step(next_state):
    state_values = next_state.astype(jnp.float32)
    summed = lax.psum(state_values, "member")
    anomaly = (state_values - summed / MEMBERS).astype(jnp.bfloat16)
    return (next_state, anomaly)


def solution(mesh):
    placed = (
        P(("groups", "spatial"), None, None),
        P(),
        P(),
        P(),
        P(),
        P(),
        P(),
        P(),
        P(),
        P(),
        P(),
        P(),
        P(),
    )
    update = jax.shard_map(
        on_device,
        mesh=mesh,
        in_specs=placed,
        out_specs=P(("groups", "spatial"), None, None),
        check_vma=False,
    )
    member_span = mesh.shape["spatial"] // MEMBERS
    ensemble_mesh = Mesh(
        mesh.devices.reshape(mesh.shape["groups"], MEMBERS, member_span),
        ("groups", "member", "half"),
    )
    member_rows = P(("groups", "member", "half"), None, None)
    spread = jax.shard_map(
        ensemble_step,
        mesh=ensemble_mesh,
        in_specs=(member_rows,),
        out_specs=(member_rows, member_rows),
        check_vma=False,
    )

    def step(*args):
        return spread(update(*args))

    return step
```
